32 devices in a mesh: gx: 4 (over z), gy: 4 (over y, core), gz: 2 (over x).
Axes of the slice: x: 2, y: 2, z: 4, core: 2. Of those that a mesh axis runs over, the one named last changes fastest.
Arguments:
- operator: bfloat16 [4, 4, 2, 1152, 1152], P('gx', 'gy', 'gz'), may hold values from -0.1875 to 0.1875
- lift: bfloat16 [4, 4, 2, 1152, 128], P('gx', 'gy', 'gz'), may hold values from -0.5 to 0.5
- source: bfloat16 [4, 4, 2, 128, 256], P('gx', 'gy', 'gz'), may hold values from -6 to 6
- traces_in: bfloat16 [4, 4, 2, 1152, 256], P('gx', 'gy', 'gz'), may hold values from -6 to 6
- depth: int32 [8], replicated, may hold values from 0 to 6
- direction: int32 [8], replicated, may hold values from 0 to 1
Outputs:
- traces_out: bfloat16 [4, 4, 2, 1152, 256], P('gx', 'gy', 'gz')
The draws below stay inside these ranges and needn't reach their ends.
All inputs are finite; a program needn't handle non-finite values.
Results may differ from the reference program's by a relative error of at most 0.008.
Values may be sent and summed in bfloat16 or wider, within the bound.
No kernel may reach another device: no remote copies, remote signals or barrier semaphores. Data moves between devices by JAX's collectives and lax.ppermute only.
A program may use at most 64 MiB of HBM per device.

```python
import jax
import jax.numpy as jnp
from jax import lax

FACE = 384
ORDER = 1152
SRC = 128
NB = 8
RB = 32
RHS = 256
STEPS = 6
N_GX = 4
N_GY = 4
N_GZ = 2


def set_ends(array, stream_key, smallest, high):
    longest = array.shape.index(max(array.shape))
    spots = []
    for shift in (0, 1):
        where = [jax.random.randint(jax.random.fold_in(stream_key, axis), (), 0, length) for axis, length in enumerate(array.shape)]
        where[longest] = (where[longest] + shift) % array.shape[longest]
        spots.append(tuple(where))
    return array.at[spots[0]].set(smallest).at[spots[1]].set(high)


def shard_levels(stream_key, dims, cuts, low, high):
    gain, own = 1.0, jax.random.fold_in(stream_key, 6)
    for axis_at, shards_of in cuts:
        draws = jnp.exp(jax.random.uniform(jax.random.fold_in(own, axis_at), (shards_of,), jnp.float32, low / len(cuts), high / len(cuts)))
        gain = gain * jnp.repeat(draws, dims[axis_at] // shards_of).reshape([-1 if axis == axis_at else 1 for axis in range(len(dims))])
    return gain


def gaussian(own_key, shape, width, limit, shards=(), kind=jnp.bfloat16):
    values = width * jax.random.normal(own_key, shape, jnp.float32)
    if shards:
        values = values * shard_levels(own_key, shape, shards, -0.22, 0.18)
    return jnp.clip(values, -limit, limit).astype(kind)


def setup_inputs(seed: int = 0) -> dict:
    seeds = jax.random.split(jax.random.key(seed), 7)
    operator = gaussian(seeds[0], (N_GX, N_GY, N_GZ, ORDER, ORDER), ORDER ** -0.5, 0.1875, ((0, 4), (1, 4), (2, 2)))
    lift = gaussian(seeds[1], (N_GX, N_GY, N_GZ, ORDER, SRC), SRC ** -0.5, 0.5, ((0, 4), (1, 4), (2, 2)))
    source = gaussian(seeds[2], (N_GX, N_GY, N_GZ, SRC, RHS), 1.0, 6.0, ((0, 4), (1, 4), (2, 2)))
    traces_in = gaussian(seeds[3], (N_GX, N_GY, N_GZ, ORDER, RHS), 1.0, 6.0, ((0, 4), (1, 4), (2, 2)))
    depth = set_ends(jax.random.randint(seeds[4], (NB,), 0, STEPS + 1), jax.random.fold_in(seeds[4], 1), 0, STEPS).astype(jnp.int32)
    direction = set_ends(jax.random.randint(seeds[5], (NB,), 0, 2), jax.random.fold_in(seeds[5], 1), 0, 1).astype(jnp.int32)
    return {"operator": operator, "lift": lift, "source": source, "traces_in": traces_in, "depth": depth, "direction": direction}


def block_product(pair):
    return jnp.dot(pair[0], pair[1], preferred_element_type=jnp.float32)


def neighbour_face(face, axis, backward):
    widths = [(0, 0)] * face.ndim
    widths[axis] = (1, 1)
    padded = jnp.pad(face, widths)
    count = face.shape[axis]
    lower = lax.slice_in_dim(padded, 0, count, axis=axis)
    upper = lax.slice_in_dim(padded, 2, count + 2, axis=axis)
    return jnp.where(backward, upper, lower)


def reference(operator, lift, source, traces_in, depth, direction):
    grid = operator.shape[:3]
    blocks = grid[0] * grid[1] * grid[2]
    flat_ops = operator.reshape(blocks, ORDER, ORDER)
    lifted = lax.map(block_product, (lift.reshape(blocks, ORDER, SRC), source.reshape(blocks, SRC, RHS)))
    backward = jnp.repeat(direction == 1, RB)
    state = traces_in
    for step in range(STEPS):
        gate = jnp.repeat(depth <= step, RB).astype(jnp.float32)
        product = lax.map(block_product, (flat_ops, state.reshape(blocks, ORDER, RHS)))
        outgoing = (product + gate * lifted).astype(jnp.bfloat16).reshape(grid + (ORDER, RHS))
        faces = []
        for axis in range(3):
            face = outgoing[:, :, :, axis * FACE:(axis + 1) * FACE, :]
            faces.append(neighbour_face(face, axis, backward))
        state = jnp.concatenate(faces, axis=3)
    return state
```

```python
import functools

import jax
import jax.numpy as jnp
from jax import lax
from jax.experimental import pallas as pl
from jax.experimental.pallas import tpu as pltpu
from jax.sharding import PartitionSpec as P

STEPS = 6
AXES = ("gx", "gy", "gz")
VMEM = pl.BlockSpec(memory_space=pltpu.VMEM)
SMEM = pl.BlockSpec(memory_space=pltpu.SMEM)


def swaps(axis):
    size = lax.axis_size(axis)
    sets = []
    for first in (0, 1):
        pairs = [(i, i + 1) for i in range(first, size - 1, 2)]
        sets.append(pairs + [(j, i) for i, j in pairs])
    return sets


def exchange(face, axis):
    return [lax.ppermute(face, axis, pairs) for pairs in swaps(axis) if pairs]


def per_column(values, width, rows):
    batches = values.shape[0]
    batch = lax.broadcasted_iota(jnp.int32, (rows, width), 1) // (width // batches)
    out = jnp.zeros((rows, width), jnp.int32)
    for b in range(batches):
        out = jnp.where(batch == b, values[b], out)
    return out


def choose(arrived, axis, direction, dtype):
    rows, width = arrived[0].shape
    even = 1 - lax.rem(lax.axis_index(axis), 2)
    first = per_column(direction, width, rows) == even
    other = arrived[1][...] if len(arrived) > 1 else jnp.zeros((rows, width), dtype)
    return jnp.where(first, arrived[0][...], other)


def step_kernel(step, counts, *refs):
    operator, lift, source, depth, direction = refs[:5]
    stack = refs[-1]
    faces = refs[-4:-1]
    arrived = refs[5:-4]
    order, width = operator.shape[0], source.shape[1]
    if step == 0:
        stack[:order, :] = arrived[0][...]
    else:
        rows = order // len(AXES)
        at = 0
        for n, axis in enumerate(AXES):
            stack[n * rows : (n + 1) * rows, :] = choose(arrived[at : at + counts[n]], axis, direction, stack.dtype)
            at += counts[n]
    injected = per_column(depth, width, source.shape[0]) <= step
    stack[order:, :] = jnp.where(injected, source[...], jnp.zeros_like(source[...]))
    rows = order // len(AXES)
    for n, face in enumerate(faces):
        total = jnp.dot(operator[n * rows : (n + 1) * rows, :], stack[:order, :], preferred_element_type=jnp.float32)
        total += jnp.dot(lift[n * rows : (n + 1) * rows, :], stack[order:, :], preferred_element_type=jnp.float32)
        face[...] = total.astype(face.dtype)


def last_kernel(counts, direction, *refs):
    out = refs[-1]
    rows = out.shape[0] // len(AXES)
    at = 0
    for n, axis in enumerate(AXES):
        out[n * rows : (n + 1) * rows, :] = choose(refs[at : at + counts[n]], axis, direction, out.dtype)
        at += counts[n]


def body(operator, lift, source, traces_in, depth, direction):
    shape = traces_in.shape
    operator, lift, source, state = operator[0, 0, 0], lift[0, 0, 0], source[0, 0, 0], traces_in[0, 0, 0]
    order, width = state.shape
    rows = order // len(AXES)
    face = jax.ShapeDtypeStruct((rows, width), state.dtype)
    counts = [sum(1 for pairs in swaps(axis) if pairs) for axis in AXES]
    params = pltpu.CompilerParams(vmem_limit_bytes=16 * 2**20)
    arrived = [state]
    for step in range(STEPS):
        faces = pl.pallas_call(
            functools.partial(step_kernel, step, counts),
            out_shape=[face] * 3,
            in_specs=[VMEM] * 3 + [SMEM] * 2 + [VMEM] * len(arrived),
            out_specs=[VMEM] * 3,
            scratch_shapes=[pltpu.VMEM((order + source.shape[0], width), state.dtype)],
            compiler_params=params,
            name=f"step{step}",
        )(operator, lift, source, depth, direction, *arrived)
        arrived = [piece for value, axis in zip(faces, AXES) for piece in exchange(value, axis)]
    state = pl.pallas_call(
        functools.partial(last_kernel, counts),
        out_shape=jax.ShapeDtypeStruct((order, width), state.dtype),
        in_specs=[SMEM] + [VMEM] * len(arrived),
        out_specs=VMEM,
        compiler_params=params,
        name="last",
    )(direction, *arrived)
    return state.reshape(shape)


def solution(mesh):
    placed = P("gx", "gy", "gz", None, None)
    return jax.shard_map(
        body,
        mesh=mesh,
        in_specs=(placed, placed, placed, placed, P(), P()),
        out_specs=placed,
        check_vma=False,
    )
```

```python
import functools

import jax
import jax.numpy as jnp
from jax import lax
from jax.experimental import pallas as pl
from jax.experimental.pallas import tpu as pltpu
from jax.sharding import PartitionSpec as P

STEPS = 6
AXES = ("gx", "gy", "gz")
FILL = {"gx": "gy", "gy": "gz", "gz": "gy"}
TILE = 16
VMEM = pl.BlockSpec(memory_space=pltpu.VMEM)
HBM = pl.BlockSpec(memory_space=pltpu.HBM)


def device(position):
    at = 0
    for axis in AXES:
        at = at * lax.axis_size(axis) + position[axis]
    return at


def devices():
    positions = [{}]
    for axis in AXES:
        positions = [dict(p, **{axis: i}) for p in positions for i in range(lax.axis_size(axis))]
    return positions


def swapped(position, axis, first):
    i = position[axis]
    j = i + 1 if (i - first) % 2 == 0 else i - 1
    return dict(position, **{axis: j}) if first <= min(i, j) and max(i, j) < lax.axis_size(axis) else None


def exchange(face, axis, first):
    pairs = []
    for position in devices():
        partner = swapped(position, axis, first) or swapped(position, FILL[axis], 0)
        if partner is not None:
            pairs.append((device(position), device(partner)))
    return lax.ppermute(face, AXES, pairs)


def sets(axis):
    return [first for first in (0, 1) if lax.axis_size(axis) > 1 + first]


def arrivals(faces):
    pieces = {}
    for axis, first in [("gx", 0), ("gx", 1), ("gz", 0), ("gz", 1), ("gy", 1), ("gy", 0)]:
        if first in sets(axis):
            pieces[axis, first] = exchange(faces[AXES.index(axis)], axis, first)
    return [pieces[axis, first] for axis in AXES for first in sets(axis)]


def choose(arrived, axis, direction):
    size, at = lax.axis_size(axis), lax.axis_index(axis)
    shape, dtype = arrived[0].shape, arrived[0].dtype
    even = (1 - lax.rem(at, 2)).astype(jnp.float32)
    toward = direction[...].astype(jnp.float32)
    first = toward * even + (1.0 - toward) * (1.0 - even)
    zeros = jnp.zeros(shape, dtype)

    def where(row, value, other):
        mask = jnp.broadcast_to(row.astype(dtype)[:1], shape)
        return jnp.where(mask > 0, value, other)

    paired = (at + (1 - 2 * lax.rem(at, 2)) < size).astype(jnp.float32)
    if len(arrived) == 1:
        return where(first * paired, arrived[0][...], zeros)
    inner = jnp.where((at > 0) & (at + 2 * lax.rem(at, 2) - 1 < size), 1.0, 0.0)
    return where(first * paired, arrived[0][...], where((1.0 - first) * inner, arrived[1][...], zeros))


def inject(source, depth, step):
    mask = jnp.broadcast_to(depth[...][:1], source.shape)
    return jnp.where(mask <= step, source[...], jnp.zeros_like(source[...]))


def multiply(operator, lift, stack, faces):
    order = operator.shape[1]
    rows = order // len(AXES)
    for n, face in enumerate(faces):
        total = jnp.dot(operator[n * rows : (n + 1) * rows, :], stack[:order, :], preferred_element_type=jnp.float32)
        total += jnp.dot(lift[n * rows : (n + 1) * rows, :], stack[order:, :], preferred_element_type=jnp.float32)
        face[...] = total.astype(face.dtype)


def row_of(values, shape):
    batches, width = values.shape[0], shape[1]
    batch = lax.broadcasted_iota(jnp.int32, shape, 1) // (width // batches)
    out = jnp.zeros(shape, jnp.int32)
    for b in range(batches):
        out = jnp.where(batch == b, values[b], out)
    return out.astype(jnp.float32)


def first_kernel(*refs):
    inputs, (face_x, face_y, face_z, operator, lift, source, depth, direction) = refs[:6], refs[6:14]
    stack, depth_s, direction_s, sems = refs[14:]
    order = operator.shape[0]
    targets = (operator, lift, source, stack.at[:order, :], depth_s, direction_s)
    copies = [pltpu.make_async_copy(a, b, sems.at[n]) for n, (a, b) in enumerate(zip(inputs, targets))]
    for copy in reversed(copies):
        copy.start()
    for copy in reversed(copies[1:]):
        copy.wait()
    depth[...] = row_of(depth_s, depth.shape).astype(depth.dtype)
    direction[...] = row_of(direction_s, direction.shape).astype(direction.dtype)
    stack[order:, :] = inject(source, depth, 0)
    copies[0].wait()
    multiply(operator, lift, stack, (face_x, face_y, face_z))


def step_kernel(step, counts, operator, lift, source, depth, direction, *refs):
    arrived, faces, stack = refs[:-4], refs[-4:-1], refs[-1]
    order = operator.shape[0]
    assemble(counts, arrived, direction, stack.at[:order, :])
    stack[order:, :] = inject(source, depth, step)
    multiply(operator, lift, stack, faces)


def assemble(counts, arrived, direction, out):
    rows = out.shape[0] // len(AXES)
    at = 0
    for n, axis in enumerate(AXES):
        if counts[n]:
            out[n * rows : (n + 1) * rows, :] = choose(arrived[at : at + counts[n]], axis, direction)
        else:
            out[n * rows : (n + 1) * rows, :] = jnp.zeros((rows, out.shape[1]), out.dtype)
        at += counts[n]


def last_kernel(counts, direction, *refs):
    assemble(counts, refs[:-1], direction, refs[-1])


def body(operator, lift, source, traces_in, depth, direction):
    shape = traces_in.shape
    operator, lift, source, state = operator[0, 0, 0], lift[0, 0, 0], source[0, 0, 0], traces_in[0, 0, 0]
    order, width = state.shape
    like = lambda value: jax.ShapeDtypeStruct(value.shape, value.dtype)
    face = jax.ShapeDtypeStruct((order // len(AXES), width), state.dtype)
    row = jax.ShapeDtypeStruct((TILE, width), state.dtype)
    stack = pltpu.VMEM((order + source.shape[0], width), state.dtype)
    counts = [len(sets(axis)) for axis in AXES]
    params = pltpu.CompilerParams(vmem_limit_bytes=16 * 2**20)
    *faces, operator, lift, source, depth, direction = pl.pallas_call(
        first_kernel,
        out_shape=[face] * 3 + [like(operator), like(lift), like(source), row, row],
        in_specs=[HBM] * 6,
        out_specs=[VMEM] * 8,
        scratch_shapes=[
            stack,
            pltpu.SMEM(depth.shape, depth.dtype),
            pltpu.SMEM(direction.shape, direction.dtype),
            pltpu.SemaphoreType.DMA((6,)),
        ],
        compiler_params=params,
        name="first",
    )(*[pltpu.with_memory_space_constraint(value, pltpu.HBM) for value in (operator, lift, source, state, depth, direction)])
    for step in range(1, STEPS):
        arrived = arrivals(faces)
        faces = pl.pallas_call(
            functools.partial(step_kernel, step, counts),
            out_shape=[face] * 3,
            in_specs=[VMEM] * (5 + len(arrived)),
            out_specs=[VMEM] * 3,
            scratch_shapes=[stack],
            compiler_params=params,
            name=f"step{step}",
        )(operator, lift, source, depth, direction, *arrived)
    arrived = arrivals(faces)
    state = pl.pallas_call(
        functools.partial(last_kernel, counts),
        out_shape=like(state),
        in_specs=[VMEM] * (1 + len(arrived)),
        out_specs=VMEM,
        compiler_params=params,
        name="last",
    )(direction, *arrived)
    return state.reshape(shape)


def solution(mesh):
    placed = P("gx", "gy", "gz", None, None)
    return jax.shard_map(
        body,
        mesh=mesh,
        in_specs=(placed, placed, placed, placed, P(), P()),
        out_specs=placed,
        check_vma=False,
    )
```

```python
import functools

import jax
import jax.numpy as jnp
from jax import lax
from jax.experimental import pallas as pl
from jax.experimental.pallas import tpu as pltpu
from jax.sharding import PartitionSpec as P

STEPS = 6
AXES = ("gx", "gy", "gz")
FILL = {"gx": "gy", "gy": "gy", "gz": "gy"}
TILE = 16
VMEM = pl.BlockSpec(memory_space=pltpu.VMEM)
HBM = pl.BlockSpec(memory_space=pltpu.HBM)


def device(position):
    at = 0
    for axis in AXES:
        at = at * lax.axis_size(axis) + position[axis]
    return at


def devices():
    positions = [{}]
    for axis in AXES:
        positions = [dict(p, **{axis: i}) for p in positions for i in range(lax.axis_size(axis))]
    return positions


def swapped(position, axis, first):
    i = position[axis]
    j = i + 1 if (i - first) % 2 == 0 else i - 1
    return dict(position, **{axis: j}) if first <= min(i, j) and max(i, j) < lax.axis_size(axis) else None


def filler(position, axis):
    if FILL[axis] == axis:
        other = lax.axis_size(axis) - 1 - position[axis]
        return dict(position, **{axis: other}) if lax.axis_size(axis) % 2 == 0 else None
    return swapped(position, FILL[axis], 0)


def exchange(face, axis, first):
    pairs = []
    for position in devices():
        partner = swapped(position, axis, first) or filler(position, axis)
        if partner is not None:
            pairs.append((device(position), device(partner)))
    return lax.ppermute(face, AXES, pairs)


def sets(axis):
    return [first for first in (0, 1) if lax.axis_size(axis) > 1 + first]


def arrivals(faces):
    pieces = {}
    for axis, first in [("gx", 0), ("gx", 1), ("gz", 0), ("gz", 1), ("gy", 1), ("gy", 0)]:
        if first in sets(axis):
            pieces[axis, first] = exchange(faces[AXES.index(axis)], axis, first)
    return [pieces[axis, first] for axis in AXES for first in sets(axis)]


def choose(arrived, axis, direction):
    size, at = lax.axis_size(axis), lax.axis_index(axis)
    shape, dtype = arrived[0].shape, arrived[0].dtype
    even = (1 - lax.rem(at, 2)).astype(jnp.float32)
    toward = direction[...].astype(jnp.float32)
    first = toward * even + (1.0 - toward) * (1.0 - even)
    zeros = jnp.zeros(shape, dtype)

    def where(row, value, other):
        mask = jnp.broadcast_to(row.astype(dtype)[:1], shape)
        return jnp.where(mask > 0, value, other)

    paired = (at + (1 - 2 * lax.rem(at, 2)) < size).astype(jnp.float32)
    if len(arrived) == 1:
        return where(first * paired, arrived[0][...], zeros)
    inner = jnp.where((at > 0) & (at + 2 * lax.rem(at, 2) - 1 < size), 1.0, 0.0)
    return where(first * paired, arrived[0][...], where((1.0 - first) * inner, arrived[1][...], zeros))


def inject(source, depth, step):
    mask = jnp.broadcast_to(depth[...][:1], source.shape)
    return jnp.where(mask <= step, source[...], jnp.zeros_like(source[...]))


def multiply(operator, lift, stack, faces):
    order = operator.shape[1]
    rows = order // len(AXES)
    for n, face in enumerate(faces):
        total = jnp.dot(operator[n * rows : (n + 1) * rows, :], stack[:order, :], preferred_element_type=jnp.float32)
        total += jnp.dot(lift[n * rows : (n + 1) * rows, :], stack[order:, :], preferred_element_type=jnp.float32)
        face[...] = total.astype(face.dtype)


def row_of(values, shape):
    batches, width = values.shape[0], shape[1]
    batch = lax.broadcasted_iota(jnp.int32, shape, 1) // (width // batches)
    out = jnp.zeros(shape, jnp.int32)
    for b in range(batches):
        out = jnp.where(batch == b, values[b], out)
    return out.astype(jnp.float32)


def first_kernel(*refs):
    inputs, (face_x, face_y, face_z, operator, lift, source, depth, direction) = refs[:6], refs[6:14]
    stack, depth_s, direction_s, sems = refs[14:]
    order = operator.shape[0]
    targets = (operator, lift, source, stack.at[:order, :], depth_s, direction_s)
    copies = [pltpu.make_async_copy(a, b, sems.at[n]) for n, (a, b) in enumerate(zip(inputs, targets))]
    for copy in reversed(copies):
        copy.start()
    for copy in reversed(copies[1:]):
        copy.wait()
    depth[...] = row_of(depth_s, depth.shape).astype(depth.dtype)
    direction[...] = row_of(direction_s, direction.shape).astype(direction.dtype)
    stack[order:, :] = inject(source, depth, 0)
    copies[0].wait()
    multiply(operator, lift, stack, (face_x, face_y, face_z))


def step_kernel(step, counts, operator, lift, source, depth, direction, *refs):
    arrived, faces, stack = refs[:-4], refs[-4:-1], refs[-1]
    order = operator.shape[0]
    assemble(counts, arrived, direction, stack.at[:order, :])
    stack[order:, :] = inject(source, depth, step)
    multiply(operator, lift, stack, faces)


def assemble(counts, arrived, direction, out):
    rows = out.shape[0] // len(AXES)
    at = 0
    for n, axis in enumerate(AXES):
        if counts[n]:
            out[n * rows : (n + 1) * rows, :] = choose(arrived[at : at + counts[n]], axis, direction)
        else:
            out[n * rows : (n + 1) * rows, :] = jnp.zeros((rows, out.shape[1]), out.dtype)
        at += counts[n]


def last_kernel(counts, direction, *refs):
    assemble(counts, refs[:-1], direction, refs[-1])


def body(operator, lift, source, traces_in, depth, direction):
    shape = traces_in.shape
    operator, lift, source, state = operator[0, 0, 0], lift[0, 0, 0], source[0, 0, 0], traces_in[0, 0, 0]
    order, width = state.shape
    like = lambda value: jax.ShapeDtypeStruct(value.shape, value.dtype)
    face = jax.ShapeDtypeStruct((order // len(AXES), width), state.dtype)
    row = jax.ShapeDtypeStruct((TILE, width), state.dtype)
    stack = pltpu.VMEM((order + source.shape[0], width), state.dtype)
    counts = [len(sets(axis)) for axis in AXES]
    params = pltpu.CompilerParams(vmem_limit_bytes=16 * 2**20)
    *faces, operator, lift, source, depth, direction = pl.pallas_call(
        first_kernel,
        out_shape=[face] * 3 + [like(operator), like(lift), like(source), row, row],
        in_specs=[HBM] * 6,
        out_specs=[VMEM] * 8,
        scratch_shapes=[
            stack,
            pltpu.SMEM(depth.shape, depth.dtype),
            pltpu.SMEM(direction.shape, direction.dtype),
            pltpu.SemaphoreType.DMA((6,)),
        ],
        compiler_params=params,
        name="first",
    )(*[pltpu.with_memory_space_constraint(value, pltpu.HBM) for value in (operator, lift, source, state, depth, direction)])
    for step in range(1, STEPS):
        arrived = arrivals(faces)
        faces = pl.pallas_call(
            functools.partial(step_kernel, step, counts),
            out_shape=[face] * 3,
            in_specs=[VMEM] * (5 + len(arrived)),
            out_specs=[VMEM] * 3,
            scratch_shapes=[stack],
            compiler_params=params,
            name=f"step{step}",
        )(operator, lift, source, depth, direction, *arrived)
    arrived = arrivals(faces)
    state = pl.pallas_call(
        functools.partial(last_kernel, counts),
        out_shape=like(state),
        in_specs=[VMEM] * (1 + len(arrived)),
        out_specs=VMEM,
        compiler_params=params,
        name="last",
    )(direction, *arrived)
    return state.reshape(shape)


def solution(mesh):
    placed = P("gx", "gy", "gz", None, None)
    return jax.shard_map(
        body,
        mesh=mesh,
        in_specs=(placed, placed, placed, placed, P(), P()),
        out_specs=placed,
        check_vma=False,
    )
```

```python
import functools

import jax
import jax.numpy as jnp
from jax import lax
from jax.experimental import pallas as pl
from jax.experimental.pallas import tpu as pltpu
from jax.sharding import PartitionSpec as P

STEPS = 6
AXES = ("gx", "gy", "gz")
FILL = {"gx": "gy", "gy": "gz", "gz": "gy"}
TILE = 16
VMEM = pl.BlockSpec(memory_space=pltpu.VMEM)
HBM = pl.BlockSpec(memory_space=pltpu.HBM)


def device(position):
    at = 0
    for axis in AXES:
        at = at * lax.axis_size(axis) + position[axis]
    return at


def devices():
    positions = [{}]
    for axis in AXES:
        positions = [dict(p, **{axis: i}) for p in positions for i in range(lax.axis_size(axis))]
    return positions


def swapped(position, axis, first):
    i = position[axis]
    j = i + 1 if (i - first) % 2 == 0 else i - 1
    return dict(position, **{axis: j}) if first <= min(i, j) and max(i, j) < lax.axis_size(axis) else None


def exchange(payload, axis, first):
    pairs = []
    for position in devices():
        partner = swapped(position, axis, first) or swapped(position, FILL[axis], 0)
        if partner is not None:
            pairs.append((device(position), device(partner)))
    return lax.ppermute(payload, AXES, pairs)


def sets():
    return [(axis, first) for axis in AXES for first in (0, 1) if lax.axis_size(axis) > 1 + first]


def fold(face, extra):
    return face[0] * extra // (face[1] // 2)


def roll(value, shift):
    shift %= value.shape[1]
    return pltpu.roll(value.astype(jnp.float32), shift, 1).astype(value.dtype) if shift else value


def pack(half, offset, extra):
    lanes = half.shape[1]
    blocks = lanes // extra
    rows = half.shape[0] // blocks
    lane = lax.broadcasted_iota(jnp.int32, (rows, lanes), 1) // extra
    out = None
    for q in range(blocks):
        piece = roll(half[q * rows : (q + 1) * rows], q * extra - offset).astype(jnp.float32)
        out = piece if out is None else jnp.where(lane == q, piece, out)
    return out.astype(half.dtype)


def unpack(packed, offset, extra):
    blocks = packed.shape[1] // extra
    return jnp.concatenate([roll(packed, offset - q * extra) for q in range(blocks)], axis=0)


def send(faces, extra, values):
    for axis, value in zip(AXES, values):
        targets = [ref for (name, _), ref in zip(sets(), faces) if name == axis]
        if not targets:
            continue
        half = value.shape[1] // 2
        up, down = [value[:, :half]], [value[:, half:]]
        if extra:
            up.append(pack(value[:, half:], 0, extra))
            down.append(pack(value[:, :half], half - extra, extra))
        even = lax.rem(lax.axis_index(axis), 2) == 0

        def store(order):
            for ref, pieces in zip(targets, order):
                row = 0
                for piece in pieces:
                    ref[row : row + piece.shape[0], :] = piece
                    row += piece.shape[0]

        pl.when(even)(lambda: store((up, down)))
        pl.when(jnp.logical_not(even))(lambda: store((down, up)))


def receive(arrived, extra, direction, out):
    rows, half = out.shape[0] // len(AXES), out.shape[1] // 2
    dtype = out.dtype
    down = direction[...].astype(jnp.float32)
    for n, axis in enumerate(AXES):
        pieces = [ref for (name, _), ref in zip(sets(), arrived) if name == axis]
        zeros = jnp.zeros((rows, half), dtype)
        if not pieces:
            for side in range(2):
                out[n * rows : (n + 1) * rows, side * half : (side + 1) * half] = zeros
            continue
        size, at = lax.axis_size(axis), lax.axis_index(axis)
        even = lax.rem(at, 2) == 0
        first, second = pieces[0], pieces[-1]

        def mask(row, side):
            row = row[:1, side * half : (side + 1) * half].astype(dtype)
            return jnp.broadcast_to(row, (rows, half)) > 0

        below = (1.0 - down) * jnp.where(at > 0, 1.0, 0.0)
        above = down * jnp.where(at < size - 1, 1.0, 0.0)

        def choose(low, high):
            base = slice(0, rows)
            low_extra = high_extra = zeros
            if extra:
                low_extra = unpack(low[rows:, :], 0, extra)
                high_extra = unpack(high[rows:, :], half - extra, extra)
            out[n * rows : (n + 1) * rows, :half] = jnp.where(
                mask(below, 0), low[base, :], jnp.where(mask(above, 0), high_extra, zeros)
            )
            out[n * rows : (n + 1) * rows, half:] = jnp.where(
                mask(above, 1), high[base, :], jnp.where(mask(below, 1), low_extra, zeros)
            )

        pl.when(even)(lambda: choose(second, first))
        pl.when(jnp.logical_not(even))(lambda: choose(first, second))


def inject(source, wait):
    mask = jnp.broadcast_to(wait[...][:1], source.shape)
    return jnp.where(mask <= 0, source[...], jnp.zeros_like(source[...]))


def multiply(operator, lift, stack):
    order = operator.shape[1]
    rows = order // len(AXES)
    faces = []
    for n in range(len(AXES)):
        total = jnp.dot(operator[n * rows : (n + 1) * rows, :], stack[:order, :], preferred_element_type=jnp.float32)
        total += jnp.dot(lift[n * rows : (n + 1) * rows, :], stack[order:, :], preferred_element_type=jnp.float32)
        faces.append(total.astype(stack.dtype))
    return faces


def spread(values, places, shape, axis):
    batches = values.shape[0]
    place = lax.broadcasted_iota(jnp.int32, shape, axis) // (shape[axis] // batches)
    out = jnp.zeros(shape, jnp.int32)
    for b in range(batches):
        out = jnp.where(place == places[b], values[b], out)
    return out


def first_kernel(extra, count, *refs):
    inputs, payloads = refs[:6], refs[6 : 6 + count]
    operator, lift, source, wait, direction, sorting = refs[6 + count : 12 + count]
    stack, raw, raw_source, depth_s, direction_s, places_s, sems = refs[12 + count :]
    order, width = operator.shape[0], raw.shape[1]
    targets = (operator, lift, raw_source, raw, depth_s, direction_s)
    copies = [pltpu.make_async_copy(a, b, sems.at[n]) for n, (a, b) in enumerate(zip(inputs, targets))]
    for copy in reversed(copies):
        copy.start()
    for copy in (copies[5], copies[4]):
        copy.wait()
    batches = depth_s.shape[0]
    ups = batches - sum(direction_s[b] for b in range(batches))
    seen = [jnp.int32(0), ups]
    for b in range(batches):
        down = direction_s[b]
        places_s[b] = jnp.where(down == 1, seen[1], seen[0])
        seen = [seen[0] + 1 - down, seen[1] + down]
    identity = list(range(batches))
    wait[...] = spread(depth_s, places_s, wait.shape, 1).astype(jnp.float32).astype(wait.dtype)
    direction[...] = spread(direction_s, places_s, direction.shape, 1).astype(jnp.float32).astype(direction.dtype)
    block = width // batches
    row = lax.broadcasted_iota(jnp.int32, (width, width), 0)
    column = lax.broadcasted_iota(jnp.int32, (width, width), 1)
    target = spread(places_s, identity, (width, width), 0) * block + lax.rem(row, block)
    sorting[...] = jnp.where(target == column, 1.0, 0.0).astype(sorting.dtype)
    for copy in (copies[3], copies[2]):
        copy.wait()
    ordered = lambda value: jnp.dot(value[...], sorting[...], preferred_element_type=jnp.float32).astype(stack.dtype)
    stack[:order, :] = ordered(raw)
    source[...] = ordered(raw_source)
    stack[order:, :] = inject(source, wait)
    wait[...] = wait[...] - 1
    for copy in (copies[1], copies[0]):
        copy.wait()
    send(payloads, extra, multiply(operator, lift, stack))


def step_kernel(extra, count, operator, lift, source, wait, direction, *refs):
    arrived, payloads, left, stack = refs[:count], refs[count:-2], refs[-2], refs[-1]
    order = operator.shape[0]
    receive(arrived, extra, direction, stack.at[:order, :])
    stack[order:, :] = inject(source, wait)
    left[...] = wait[...] - 1
    send(payloads, extra, multiply(operator, lift, stack))


def last_kernel(extra, direction, sorting, *refs):
    arrived, out, stack = refs[:-2], refs[-2], refs[-1]
    receive(arrived, extra, direction, stack)
    back = lax.dot_general(stack[...], sorting[...], (((1,), (1,)), ((), ())), preferred_element_type=jnp.float32)
    out[...] = back.astype(out.dtype)


def exchanges(payloads):
    pieces = {}
    order = [("gx", 0), ("gx", 1), ("gz", 0), ("gz", 1), ("gy", 1), ("gy", 0)]
    for key in order:
        if key in sets():
            pieces[key] = exchange(payloads[sets().index(key)], *key)
    return [pieces[key] for key in sets()]


def program(extra, operator, lift, source, state, depth, direction):
    order, width = state.shape
    dtype = state.dtype
    like = lambda value: jax.ShapeDtypeStruct(value.shape, value.dtype)
    face = (order // len(AXES), width)
    payload = jax.ShapeDtypeStruct((face[0] + fold(face, extra), width // 2), dtype)
    row = jax.ShapeDtypeStruct((TILE, width), dtype)
    stack = pltpu.VMEM((order + source.shape[0], width), dtype)
    count = len(sets())
    params = pltpu.CompilerParams(vmem_limit_bytes=16 * 2**20)
    inputs = [pltpu.with_memory_space_constraint(v, pltpu.HBM) for v in (operator, lift, source, state, depth, direction)]
    outputs = pl.pallas_call(
        functools.partial(first_kernel, extra, count),
        out_shape=[payload] * count
        + [like(operator), like(lift), like(source), row, row, jax.ShapeDtypeStruct((width, width), dtype)],
        in_specs=[HBM] * 6,
        out_specs=[VMEM] * (count + 6),
        scratch_shapes=[
            stack,
            pltpu.VMEM(state.shape, dtype),
            pltpu.VMEM(source.shape, dtype),
            pltpu.SMEM(depth.shape, depth.dtype),
            pltpu.SMEM(direction.shape, direction.dtype),
            pltpu.SMEM(direction.shape, direction.dtype),
            pltpu.SemaphoreType.DMA((6,)),
        ],
        compiler_params=params,
        name="first",
    )(*inputs)
    payloads, (operator, lift, source, wait, direction, sorting) = outputs[:count], outputs[count:]
    advance = pl.pallas_call(
        functools.partial(step_kernel, extra, count),
        out_shape=[payload] * count + [row],
        in_specs=[VMEM] * (5 + count),
        out_specs=[VMEM] * (count + 1),
        scratch_shapes=[stack],
        compiler_params=params,
        name="step",
    )
    for _ in range(1, STEPS):
        *payloads, wait = advance(operator, lift, source, wait, direction, *exchanges(payloads))
    arrived = exchanges(payloads)
    return pl.pallas_call(
        functools.partial(last_kernel, extra),
        out_shape=like(state),
        in_specs=[VMEM] * (2 + count),
        out_specs=VMEM,
        scratch_shapes=[pltpu.VMEM(state.shape, dtype)],
        compiler_params=params,
        name="last",
    )(direction, sorting, *arrived)


def levels(batches):
    out = [1]
    while out[-1] < batches // 2:
        out.append(2 * out[-1])
    return out


def body(operator, lift, source, traces_in, depth, direction):
    batches, width = direction.shape[0], traces_in.shape[-1]
    state = traces_in[0, 0, 0]
    sizes = levels(batches)
    excess = jnp.abs(jnp.sum(direction) - batches // 2)
    level = sum((excess > size).astype(jnp.int32) for size in sizes[:-1])
    branches = [functools.partial(program, size * (width // batches)) for size in sizes]
    state = lax.switch(level, branches, operator[0, 0, 0], lift[0, 0, 0], source[0, 0, 0], state, depth, direction)
    return state.reshape(traces_in.shape)


def solution(mesh):
    placed = P("gx", "gy", "gz", None, None)
    return jax.shard_map(
        body,
        mesh=mesh,
        in_specs=(placed, placed, placed, placed, P(), P()),
        out_specs=placed,
        check_vma=False,
    )
```

```python
import functools

import jax
import jax.numpy as jnp
from jax import lax
from jax.experimental import pallas as pl
from jax.experimental.pallas import tpu as pltpu
from jax.sharding import PartitionSpec as P

STEPS = 6
AXES = ("gx", "gy", "gz")
PAIR = "gy"
ORDER = ("gz", "gx", "gy")
LANES = 128
TILE = 16
VMEM = pl.BlockSpec(memory_space=pltpu.VMEM)
SMEM = pl.BlockSpec(memory_space=pltpu.SMEM)
HBM = pl.BlockSpec(memory_space=pltpu.HBM)


def device(position):
    at = 0
    for axis in AXES:
        at = at * lax.axis_size(axis) + position[axis]
    return at


def devices():
    positions = [{}]
    for axis in AXES:
        positions = [dict(p, **{axis: i}) for p in positions for i in range(lax.axis_size(axis))]
    return positions


def mate(position):
    return dict(position, **{PAIR: position[PAIR] ^ 1})


def onward(position, axis):
    step = (2 if axis == PAIR else 1) * (1 if position[PAIR] % 2 == 0 else -1)
    there = position[axis] + step
    return dict(position, **{axis: there}) if 0 <= there < lax.axis_size(axis) else mate(position)


def permute(value, target):
    return lax.ppermute(value, AXES, [(device(p), device(target(p))) for p in devices()])


def pass_on(payloads):
    pieces = {}
    for axis in ORDER:
        pieces[axis] = permute(payloads[AXES.index(axis)], functools.partial(onward, axis=axis))
    return [pieces[axis] for axis in AXES]


def behind(axis, dtype):
    at = lax.axis_index(axis)
    down = lax.rem(lax.axis_index(PAIR), 2)
    there = at - 1 + 2 * down
    return jnp.where((there >= 0) & (there < lax.axis_size(axis)), 1.0, 0.0).astype(dtype)


def inject(source, wait):
    gate = jnp.concatenate([wait[...]] * (source.shape[1] // LANES), axis=1)
    return jnp.where(gate <= 0, source[...], jnp.zeros_like(source[...]))


def across(a, b):
    return lax.dot_general(a, b, (((1,), (1,)), ((), ())), preferred_element_type=jnp.float32)


def spread(values, origins, out):
    batches = values.shape[0]
    block = out.shape[0] // batches
    for place in range(batches):
        number = values[origins[place]].astype(jnp.float32)
        out[place * block : (place + 1) * block, :] = jnp.full((block, out.shape[1]), number).astype(out.dtype)


def first_kernel(held, *refs):
    operator_h, lift_h, *inputs = refs[:6]
    outgoing, operator, lift, source, wait, direction, sorting, level = refs[6:14]
    stack, raw, raw_source, depth_s, direction_s, origins_s, sems = refs[14:]
    order, width = raw.shape
    rows = order // len(AXES)
    dtype = stack.dtype
    parts = [slice(n * rows, (n + 1) * rows) for n in range(len(AXES))]
    moves = list(zip(inputs[::-1], (direction_s, depth_s, raw, raw_source)))
    for part in parts:
        moves.append((operator_h.at[part, :], operator.at[part, :]))
        moves.append((lift_h.at[part, :], lift.at[part, :]))
    copies = [pltpu.make_async_copy(a, b, sems.at[n]) for n, (a, b) in enumerate(moves)]
    for copy in copies:
        copy.start()
    copies[0].wait()
    copies[1].wait()
    batches = depth_s.shape[0]
    downs = sum(direction_s[b] for b in range(batches))
    most = jnp.maximum(downs, batches - downs)
    level[0] = sum((most > size).astype(jnp.int32) for size in held[:-1])
    seen = [jnp.int32(0), batches - downs]
    for b in range(batches):
        down = direction_s[b]
        origins_s[jnp.where(down == 1, seen[1], seen[0])] = b
        seen = [seen[0] + 1 - down, seen[1] + down]
    spread(depth_s, origins_s, wait)
    spread(direction_s, origins_s, direction)
    block = width // batches
    ahead = lax.broadcasted_iota(jnp.int32, (block, width), 1) - lax.broadcasted_iota(jnp.int32, (block, width), 0)
    for place in range(batches):
        picked = jnp.where(ahead == origins_s[place] * block, 1.0, 0.0)
        sorting[place * block : (place + 1) * block, :] = picked.astype(dtype)
    copies[2].wait()
    stack[:, :order] = across(sorting[...], raw[...]).astype(dtype)
    copies[3].wait()
    source[...] = across(sorting[...], raw_source[...]).astype(dtype)
    stack[:, order:] = inject(source, wait)
    for n, part in enumerate(parts):
        copies[4 + 2 * n].wait()
        copies[5 + 2 * n].wait()
        total = across(stack[:, :order], operator[part, :]) + across(stack[:, order:], lift[part, :])
        outgoing[:, part] = total.astype(dtype)


def store(own, other, payloads, keep):
    height, rows = keep.shape
    for n, axis in enumerate(AXES):
        part = slice(n * rows, (n + 1) * rows)
        if axis == PAIR:
            keep[...] = own[:, part]
            payloads[n][...] = other[:, part]
        else:
            payloads[n][:height, :] = own[:, part]
            payloads[n][height:, :] = other[:, part]


def second_kernel(outgoing, operator, lift, raw_source, raw, sorting, source, wait, *refs):
    payloads, (keep, source_own, source_other, left) = refs[:3], refs[3:]
    height, width = keep.shape[0], outgoing.shape[0]
    dtype = outgoing.dtype
    start = lax.rem(lax.axis_index(PAIR), 2) * (width - height)
    mine = pl.ds(pl.multiple_of(start, TILE), height)
    picked = sorting[mine, :]
    state = across(picked, raw[...]).astype(dtype)
    source_own[...] = source[mine, :]
    source_other[...] = across(picked, raw_source[...]).astype(dtype)
    left[...] = wait[mine, :]
    other = across(state, operator[...]) + across(inject(source_other, left), lift[...])
    left[...] = left[...] - 1
    store(outgoing[mine, :], other.astype(dtype), payloads, keep)


def early_kernel(own_operator, own_lift, other_operator, other_lift, own_source, other_source, wait, keep, y, z, *refs):
    own_total, other_total, left = refs
    height, rows = keep.shape
    dtype = keep.dtype
    y_in = y[...] * behind("gy", dtype)
    near = behind("gz", dtype)
    for total, operator, lift, source, first, at in (
        (own_total, own_operator, own_lift, own_source, y_in, 0),
        (other_total, other_operator, other_lift, other_source, keep[...], height),
    ):
        stack = jnp.concatenate([first, z[at : at + height, :] * near], axis=1)
        total[...] = across(stack, operator[:, rows:]) + across(inject(source, wait), lift[...])
    left[...] = wait[...] - 1


def late_kernel(own_operator, other_operator, own_total, other_total, x, *refs):
    payloads, keep = refs[:3], refs[3]
    height, rows = keep.shape
    dtype = keep.dtype
    near = behind("gx", dtype)
    outgoing = []
    for total, operator, at in ((own_total, own_operator, 0), (other_total, other_operator, height)):
        share = across(x[at : at + height, :] * near, operator[:, :rows])
        outgoing.append((total[...] + share).astype(dtype))
    store(*outgoing, payloads, keep)


def other_kernel(keep, x, z, out):
    height, rows = keep.shape
    dtype = keep.dtype
    out[:, :rows] = x[height:, :] * behind("gx", dtype)
    out[:, rows : 2 * rows] = keep[...]
    out[:, 2 * rows :] = z[height:, :] * behind("gz", dtype)


def last_kernel(direction, sorting, x, y, z, given, target, stack, out, sems):
    width, order = stack.shape
    height, rows = given.shape[0], order // len(AXES)
    start = width - height
    dtype = stack.dtype
    upward = lax.rem(lax.axis_index(PAIR), 2) == 0
    copies = []
    for n, (axis, face) in enumerate(zip(AXES, (x, y, z))):
        part = slice(n * rows, (n + 1) * rows)
        near = behind(axis, dtype)

        def assemble(low, high, part=part):
            if start:
                stack[:start, part] = low(0, start)
                stack[height:, part] = high(height - start, height)
            if height > start:
                down = jnp.concatenate([direction[start:height, :]] * (rows // LANES), axis=1) > 0
                stack[start:height, part] = jnp.where(down, high(0, height - start), low(start, height))

        own = lambda a, b, face=face, near=near: face[a:b, :] * near
        mates = lambda a, b, part=part: given[a:b, part]
        pl.when(upward)(functools.partial(assemble, own, mates))
        pl.when(jnp.logical_not(upward))(functools.partial(assemble, mates, own))
        back = lax.dot_general(stack[:, part], sorting[...], (((0,), (0,)), ((), ())), preferred_element_type=jnp.float32)
        out[part, :] = back.astype(dtype)
        copies.append(pltpu.make_async_copy(out.at[part, :], target.at[part, :], sems.at[n]))
        copies[-1].start()
    for copy in copies:
        copy.wait()


def shaped(dtype):
    return lambda *dims: jax.ShapeDtypeStruct(dims, dtype)


def call(kernel, outputs, operands, scratch=(), specs=None, sources=None):
    return pl.pallas_call(
        kernel,
        out_shape=outputs,
        in_specs=sources or [VMEM] * len(operands),
        out_specs=specs or [VMEM] * len(outputs),
        scratch_shapes=list(scratch),
        compiler_params=pltpu.CompilerParams(vmem_limit_bytes=16 * 2**20),
    )(*operands)


def begin(arguments, held):
    operator, lift, source, state, depth, direction = arguments
    order, width = state.shape
    inner = order + source.shape[0]
    dtype = state.dtype
    shape = shaped(dtype)
    return call(
        functools.partial(first_kernel, held),
        [shape(width, order), shape(*operator.shape), shape(*lift.shape), shape(width, source.shape[0])]
        + [shape(width, LANES)] * 2
        + [shape(width, width), jax.ShapeDtypeStruct((1,), jnp.int32)],
        [pltpu.with_memory_space_constraint(value, pltpu.HBM) for value in arguments],
        [
            pltpu.VMEM((width, inner), dtype),
            pltpu.VMEM(state.shape, dtype),
            pltpu.VMEM(source.shape, dtype),
            pltpu.SMEM(depth.shape, depth.dtype),
            pltpu.SMEM(direction.shape, direction.dtype),
            pltpu.SMEM(direction.shape, direction.dtype),
            pltpu.SemaphoreType.DMA((4 + 2 * len(AXES),)),
        ],
        [VMEM] * 7 + [SMEM],
        [HBM] * 6,
    )


def finish(height, kept, others):
    outgoing, operator, lift, source, wait, direction, sorting = kept
    other_operator, other_lift, other_source, other_state = others
    width, order = outgoing.shape
    rows, inner = order // len(AXES), source.shape[1]
    dtype = operator.dtype
    shape = shaped(dtype)
    payloads = [shape(height if axis == PAIR else 2 * height, rows) for axis in AXES]
    keep, thin, row = shape(height, rows), shape(height, inner), shape(height, LANES)
    total = jax.ShapeDtypeStruct((height, order), jnp.float32)
    *outs, keep_now, source, other_source, wait = call(
        second_kernel,
        payloads + [keep, thin, thin, row],
        [outgoing, other_operator, other_lift, other_source, other_state, sorting, source, wait],
    )
    for _ in range(1, STEPS):
        x, y, z = pass_on(outs)
        own_total, other_total, wait = call(
            early_kernel,
            [total, total, row],
            [operator, lift, other_operator, other_lift, source, other_source, wait, keep_now, y, z],
        )
        *outs, keep_now = call(late_kernel, payloads + [keep], [operator, other_operator, own_total, other_total, x])
    x, y, z = pass_on(outs)
    (given,) = call(other_kernel, [shape(height, order)], [keep_now, x, z])
    given = permute(given, mate)
    (state,) = call(
        last_kernel,
        [pltpu.HBM((order, width), dtype)],
        [direction, sorting, x, y, z, given],
        [
            pltpu.VMEM((width, order), dtype),
            pltpu.VMEM((order, width), dtype),
            pltpu.SemaphoreType.DMA((len(AXES),)),
        ],
        [HBM],
    )
    return state


def levels(batches):
    extra = [1]
    while extra[-1] < batches // 2:
        extra.append(2 * extra[-1])
    return [batches - batches // 2 + e for e in extra]


def body(operator, lift, source, traces_in, depth, direction):
    batches, width = direction.shape[0], traces_in.shape[-1]
    held = levels(batches)
    own = [value[0, 0, 0] for value in (operator, lift, source, traces_in)]
    others = [permute(value, mate) for value in own]
    *kept, level = begin([*own, depth, direction], held)
    branches = [functools.partial(finish, size * (width // batches)) for size in held]
    return lax.switch(level[0], branches, kept, others).reshape(traces_in.shape)


def solution(mesh):
    placed = P("gx", "gy", "gz", None, None)
    return jax.shard_map(
        body,
        mesh=mesh,
        in_specs=(placed, placed, placed, placed, P(), P()),
        out_specs=placed,
        check_vma=False,
    )
```
